256 devices in a mesh: sub: 4 (over x), row: 16 (over z, core), col: 4 (over y).
Axes of the slice: x: 4, y: 4, z: 8, core: 2. Of those that a mesh axis runs over, the one named last changes fastest.
Arguments:
- leaf_rhs: bfloat16 [4, 64, 4, 64, 256], P('sub', 'row', 'col'), may hold values from -6 to 6
- leaf_inverse: bfloat16 [4, 64, 4, 256, 256], P('sub', 'row', 'col'), may hold values from -0.5 to 0.5
- coupling: bfloat16 [4, 16, 64, 4, 256, 256], P('sub', 'row', None, 'col'), may hold values from -0.01171875 to 0.01171875
- pattern: int32 [4, 16, 64, 4], P('sub', 'row', None, 'col'), may hold values 0 or 1
- top_rhs: bfloat16 [16, 64, 256], replicated, may hold values from -6 to 6
- top_inverse: bfloat16 [16, 256, 256], replicated, may hold values from -0.5 to 0.5
- top_factor: bfloat16 [16, 16, 256, 256], P('row', 'col'), may hold values from -0.09375 to 0.09375
Outputs:
- leaf_solution: bfloat16 [4, 64, 4, 64, 256], P('sub', 'row', 'col')
- top_solution: bfloat16 [16, 64, 256], P('row')
The draws below stay inside these ranges and needn't reach their ends.
All inputs are finite; a program needn't handle non-finite values. No bound on the sum of `pattern` on one device may be relied on, other than what follows from the above.
Results may differ from the reference program's by a relative error of at most 0.025.
Values may be sent and summed in bfloat16 or wider, within the bound.
No kernel may reach another device: no remote copies, remote signals or barrier semaphores. Data moves between devices by JAX's collectives and lax.ppermute only.
A program may use at most 128 MiB of HBM per device.

```python
import jax
import jax.numpy as jnp
from jax import lax

B = 256
NRHS = 64
KT = 16
SUBTREES = 4
LCOLS = 4
NLC = 64


def set_ends(array, rng, low, high):
    index_at = [jax.random.randint(jax.random.fold_in(rng, axis), (), 0, length) for axis, length in enumerate(array.shape)]
    widest = array.shape.index(max(array.shape))
    beside = index_at[:widest] + [(index_at[widest] + 1) % array.shape[widest]] + index_at[widest + 1:]
    return array.at[tuple(index_at)].set(low).at[tuple(beside)].set(high)


def levels(key, shape, pieces, smallest, largest):
    gain = 1.0
    for position, shards_of in pieces:
        draws = jax.random.uniform(jax.random.fold_in(jax.random.fold_in(key, 6), position), (shards_of,), jnp.float32, smallest / len(pieces), largest / len(pieces))
        gain = gain * jnp.repeat(jnp.exp(draws), shape[position] // shards_of).reshape((-1,) + (1,) * (len(shape) - 1 - position))
    return gain


def centred(key, dims, width, bound, pieces=(), dtype=jnp.bfloat16):
    result = jax.random.normal(key, dims, jnp.float32) * width
    if len(pieces) > 0:
        result = levels(key, dims, pieces, -0.22, 0.18) * result
    return jnp.clip(result, min=-bound, max=bound).astype(dtype)


def setup_inputs(seed: int = 0) -> dict:
    key_list = jax.random.split(jax.random.key(seed), 8)
    leaf_rhs = centred(key_list[0], (SUBTREES, NLC, LCOLS, NRHS, B), 1.0, 6.0, ((0, 4), (1, 16), (2, 4)))
    leaf_inverse = centred(key_list[1], (SUBTREES, NLC, LCOLS, B, B), (B // 2) ** -0.5, 0.5, ((0, 4), (1, 16), (2, 4)))
    coupling = centred(key_list[2], (SUBTREES, KT, NLC, LCOLS, B, B), (B * NLC * LCOLS * SUBTREES) ** -0.5, 0.01171875, ((0, 4), (1, 16), (3, 4)))
    pattern = set_ends((jax.random.randint(key_list[3], (SUBTREES, KT, NLC, LCOLS), 0, 3) < 2).astype(jnp.int32), jax.random.fold_in(key_list[3], 1), 0, 1)
    top_rhs = centred(key_list[4], (KT, NRHS, B), 1.0, 6.0)
    top_inverse = centred(key_list[5], (KT, B, B), (B // 2) ** -0.5, 0.5)
    top_factor = centred(key_list[6], (KT, KT, B, B), (B * KT) ** -0.5, 0.09375, ((0, 16), (1, 4)))
    return {"leaf_rhs": leaf_rhs, "leaf_inverse": leaf_inverse, "coupling": coupling, "pattern": pattern, "top_rhs": top_rhs, "top_inverse": top_inverse, "top_factor": top_factor}


def reference(leaf_rhs, leaf_inverse, coupling, pattern, top_rhs, top_inverse, top_factor):
    leaf_tri = jnp.tril(leaf_inverse)
    leaf_forward = jnp.einsum('sicnb,sicdb->sicnd', leaf_rhs.astype(jnp.float32), leaf_tri.astype(jnp.float32)).astype(jnp.bfloat16)
    weights = pattern.astype(jnp.bfloat16)

    def updates_of(block_id):
        def one_subtree(sub_id):
            blocks = coupling[sub_id, block_id] * weights[sub_id, block_id][:, :, None, None]
            flat_left = jnp.transpose(leaf_forward[sub_id], (2, 0, 1, 3)).reshape(NRHS, -1)
            flat_right = jnp.transpose(blocks, (2, 0, 1, 3)).reshape(B, -1)
            return jnp.dot(flat_left, flat_right.T, preferred_element_type=jnp.float32)
        return jnp.sum(lax.map(one_subtree, jnp.arange(SUBTREES)), axis=0)

    updates = lax.map(updates_of, jnp.arange(KT))
    forward_rows = []
    for block_id in range(KT):
        summed = top_rhs[block_id].astype(jnp.float32) - updates[block_id]
        for earlier in range(block_id):
            summed = summed - jnp.dot(forward_rows[earlier], top_factor[block_id, earlier].T, preferred_element_type=jnp.float32)
        residue = summed.astype(jnp.bfloat16)
        forward_rows.append(jnp.dot(residue, jnp.tril(top_inverse[block_id]).T, preferred_element_type=jnp.float32).astype(jnp.bfloat16))
    solved_rows = [None] * KT
    for block_id in reversed(range(KT)):
        summed = forward_rows[block_id].astype(jnp.float32)
        for later in range(block_id + 1, KT):
            summed = summed - jnp.dot(solved_rows[later], top_factor[later, block_id], preferred_element_type=jnp.float32)
        residue = summed.astype(jnp.bfloat16)
        solved_rows[block_id] = jnp.dot(residue, jnp.tril(top_inverse[block_id]), preferred_element_type=jnp.float32).astype(jnp.bfloat16)
    top_solution = jnp.stack(solved_rows)
    flat_solution = jnp.transpose(top_solution, (1, 0, 2)).reshape(NRHS, KT * B)

    def back_of(sub_id):
        blocks = coupling[sub_id] * weights[sub_id][:, :, :, None, None]
        flat_blocks = jnp.transpose(blocks, (0, 3, 1, 2, 4)).reshape(KT * B, -1)
        product = jnp.dot(flat_solution, flat_blocks, preferred_element_type=jnp.float32)
        return jnp.transpose(product.reshape(NRHS, NLC, LCOLS, B), (1, 2, 0, 3))

    back_sums = lax.map(back_of, jnp.arange(SUBTREES))
    leaf_residue = (leaf_forward.astype(jnp.float32) - back_sums).astype(jnp.bfloat16)
    leaf_solution = jnp.einsum('sicnb,sicbd->sicnd', leaf_residue.astype(jnp.float32), leaf_tri.astype(jnp.float32)).astype(jnp.bfloat16)
    return leaf_solution, top_solution
```

```python
import jax
import jax.numpy as jnp
from jax import lax
from jax.experimental import pallas as pl
from jax.experimental.pallas import tpu as pltpu
from jax.sharding import Mesh, PartitionSpec as P

BF = jnp.bfloat16
F32 = jnp.float32
ROW = ("z", "core")
SWAP = [(0, 1), (1, 0)]
NT = (((1,), (1,)), ((), ()))
NN = (((1,), (0,)), ((), ()))


def slot(a, b, rows, cols, per):
    c, j = divmod(b, per)
    half = per // 2
    if j < half:
        return (a * cols + c) * half + j
    return ((rows - 1 - a) * cols + cols - 1 - c) * half + j - half


def top_kernel(slots, r_ref, u_ref, g_ref, f_ref, x_ref, zs):
    count = r_ref.shape[0]

    def dot(a, b, dims):
        return lax.dot_general(a, b, dims, preferred_element_type=F32)

    def rhs(k):
        return r_ref[k].astype(F32) - u_ref[k].astype(F32)

    summed = rhs(0)
    for k in range(count):
        z = dot(summed.astype(BF), g_ref[k], NT).astype(BF)
        zs[k] = z
        if k + 1 < count:
            later = rhs(k + 1)
            for b in range(k):
                later -= dot(zs[b], f_ref[slots[k + 1, b]], NT)
            summed = later - dot(z, f_ref[slots[k + 1, k]], NT)
    summed = zs[count - 1].astype(F32)
    for k in reversed(range(count)):
        x = dot(summed.astype(BF), g_ref[k], NN).astype(BF)
        x_ref[k] = x
        if k > 0:
            later = zs[k - 1].astype(F32)
            for a in range(count - 1, k, -1):
                later -= dot(x_ref[a], f_ref[slots[a, k - 1]], NN)
            summed = later - dot(x, f_ref[slots[k, k - 1]], NN)


def top_solve(slots, rhs, updates, inverse, factor):
    whole = pl.BlockSpec(memory_space=pltpu.VMEM)
    return pl.pallas_call(
        lambda *refs: top_kernel(slots, *refs),
        out_shape=jax.ShapeDtypeStruct(rhs.shape, BF),
        in_specs=[whole] * 4,
        out_specs=whole,
        scratch_shapes=[pltpu.VMEM(rhs.shape, BF)],
        compiler_params=pltpu.CompilerParams(vmem_limit_bytes=56 << 20),
        name="top_solve",
    )(rhs, updates, inverse, factor)


def sum_over(value, axis, size):
    value = value.astype(BF)
    got = [value] + [
        lax.ppermute(value, axis, [(i, (i + k) % size) for i in range(size)])
        for k in range(1, size)
    ]
    got = [g.astype(F32) for g in got]
    return (got[0] + got[2]) + (got[1] + got[3])


def build(mesh):
    subs, zs, cores, cols = mesh.devices.shape

    def local(leaf_rhs, leaf_inverse, coupling, pattern, top_rhs, top_inverse, top_factor):
        core = lax.axis_index("core")
        col = lax.axis_index("col")
        row = lax.axis_index("z") * cores + core
        own_rhs = leaf_rhs[0, :, 0]
        own_inverse = jnp.tril(leaf_inverse[0, :, 0])
        coupled = coupling[0, 0, :, 0]
        weights = pattern[0, 0, :, 0].astype(BF)
        leaves, nrhs, size = own_rhs.shape
        rows = zs * cores
        per = top_factor.shape[1]
        half = per // 2
        slots = {
            (a, b): slot(a, b, rows, cols, per) for a in range(rows) for b in range(a)
        }

        blocks = top_factor[0]
        pairs = [
            (i, rows * cols - 1 - i)
            for i in range(rows * cols)
            if i // cols - per * (i % cols) > half
        ]
        moved = lax.ppermute(blocks[half:], ("z", "core", "col"), pairs)
        shard = jnp.where(row - per * col <= 0, moved, blocks[:half])
        factor = lax.all_gather(shard, ("z", "core", "col"), axis=0, tiled=True)
        top_tri = jnp.tril(top_inverse)

        leaf_forward = jnp.einsum(
            "inb,idb->ind", own_rhs, own_inverse, preferred_element_type=F32
        ).astype(BF)
        mine = lax.all_to_all(
            jnp.broadcast_to(leaf_forward[None], (zs,) + leaf_forward.shape),
            "z", 0, 0, tiled=True,
        )
        other = lax.ppermute(mine, "core", SWAP)
        first = core == 0
        forward = jnp.stack(
            [jnp.where(first, mine, other), jnp.where(first, other, mine)], axis=1
        ).reshape(rows * leaves, nrhs, size)
        partial = jnp.einsum(
            "inb,ieb->ne", forward * weights[:, None, None], coupled,
            preferred_element_type=F32,
        )
        update = sum_over(sum_over(partial, "sub", subs), "col", cols).astype(BF)
        updates = lax.all_gather(update, ROW, axis=0)

        solution = top_solve(slots, top_rhs, updates, top_tri, factor)
        own_top = lax.dynamic_index_in_dim(solution, row, 0, keepdims=False)

        back = jnp.einsum(
            "ine,ieb->inb", own_top[None] * weights[:, None, None], coupled,
            preferred_element_type=F32,
        ).astype(BF).reshape(zs, cores, leaves, nrhs, size)
        mine = jnp.where(first, back[:, 0], back[:, 1])
        other = lax.ppermute(jnp.where(first, back[:, 1], back[:, 0]), "core", SWAP)
        pair = (mine.astype(F32) + other.astype(F32)).astype(BF)
        spread = lax.all_to_all(pair, "z", 0, 0, tiled=True)
        back_sums = jnp.sum(spread.astype(F32), axis=0)
        leaf_residue = (leaf_forward.astype(F32) - back_sums).astype(BF)
        leaf_result = jnp.einsum(
            "inb,ibd->ind", leaf_residue, own_inverse, preferred_element_type=F32
        ).astype(BF)
        return leaf_result[None, :, None], own_top[None]

    return local


def solution(mesh):
    subs, rows, cols = (mesh.shape[name] for name in ("sub", "row", "col"))
    mesh = Mesh(
        mesh.devices.reshape(subs, rows // 2, 2, cols), ("sub", "z", "core", "col")
    )
    placed = (
        P("sub", ROW, "col", None, None),
        P("sub", ROW, "col", None, None),
        P("sub", ROW, None, "col", None, None),
        P("sub", ROW, None, "col"),
        P(),
        P(),
        P(ROW, "col", None, None),
    )
    return jax.shard_map(
        build(mesh),
        mesh=mesh,
        in_specs=placed,
        out_specs=(P("sub", ROW, "col", None, None), P(ROW, None, None)),
        check_vma=False,
    )
```

```python
import jax
import jax.numpy as jnp
from jax import lax
from jax.experimental import pallas as pl
from jax.experimental.pallas import tpu as pltpu
from jax.sharding import Mesh, PartitionSpec as P

BF = jnp.bfloat16
F32 = jnp.float32
ROW = ("z", "core")
SWAP = [(0, 1), (1, 0)]
NT = (((1,), (1,)), ((), ()))
NN = (((1,), (0,)), ((), ()))


def first_block(a):
    return a * (a - 1) // 2


def top_kernel(units, r_ref, u_ref, g_ref, f_hbm, x_ref, zs, fac, sems):
    count = r_ref.shape[0]
    half = f_hbm.shape[1]

    def dot(a, b, dims):
        return lax.dot_general(a, b, dims, preferred_element_type=F32)

    def rhs(k):
        return r_ref[k].astype(F32) - u_ref[k].astype(F32)

    def block(a, b):
        return fac[first_block(a) + b]

    for a in range(1, count):
        for b in range(a):
            for part, unit in enumerate(units(a, b)):
                pltpu.make_async_copy(
                    f_hbm.at[unit],
                    fac.at[first_block(a) + b, pl.ds(part * half, half)],
                    sems.at[a],
                ).start()

    summed = rhs(0)
    for k in range(count):
        z = dot(summed.astype(BF), g_ref[k], NT).astype(BF)
        zs[k] = z
        if k + 1 < count:
            row = fac.at[pl.ds(first_block(k + 1), k + 1)]
            pltpu.make_async_copy(row, row, sems.at[k + 1]).wait()
            later = rhs(k + 1)
            for b in range(k):
                later -= dot(zs[b], block(k + 1, b), NT)
            summed = later - dot(z, block(k + 1, k), NT)
    summed = zs[count - 1].astype(F32)
    for k in reversed(range(count)):
        x = dot(summed.astype(BF), g_ref[k], NN).astype(BF)
        x_ref[k] = x
        if k > 0:
            later = zs[k - 1].astype(F32)
            for a in range(count - 1, k, -1):
                later -= dot(x_ref[a], block(a, k - 1), NN)
            summed = later - dot(x, block(k, k - 1), NN)


def top_solve(units, rhs, updates, inverse, factor):
    whole = pl.BlockSpec(memory_space=pltpu.VMEM)
    count, nrhs, size = rhs.shape
    return pl.pallas_call(
        lambda *refs: top_kernel(units, *refs),
        out_shape=jax.ShapeDtypeStruct(rhs.shape, BF),
        in_specs=[whole] * 3 + [pl.BlockSpec(memory_space=pl.ANY)],
        out_specs=whole,
        scratch_shapes=[
            pltpu.VMEM(rhs.shape, BF),
            pltpu.VMEM((first_block(count), size, size), BF),
            pltpu.SemaphoreType.DMA((count,)),
        ],
        compiler_params=pltpu.CompilerParams(vmem_limit_bytes=40 << 20),
        name="top_solve",
    )(rhs, updates, inverse, factor)


def back_kernel(where_ref, w_ref, x_ref, c_ref, mine_ref, other_ref):
    z = pl.program_id(0)
    core = where_ref[1]
    leaves = mine_ref.shape[0]
    for out, part in ((other_ref, 1 - core), (mine_ref, core)):
        for leaf in range(leaves):
            at = part * leaves + leaf
            weight = w_ref[z * 2 * leaves + at].astype(F32)
            value = lax.dot_general(
                x_ref[...], c_ref[at], NN, preferred_element_type=F32
            )
            out[leaf] = (value * weight).astype(BF)


def back_products(solution, coupled, pattern, row, core, zs, leaves):
    _, nrhs, size = solution.shape
    spec = pl.BlockSpec((None, leaves, nrhs, size), lambda z, *_: (z, 0, 0, 0))
    out = jax.ShapeDtypeStruct((zs, leaves, nrhs, size), BF)
    return pl.pallas_call(
        back_kernel,
        out_shape=(out, out),
        grid_spec=pltpu.PrefetchScalarGridSpec(
            num_scalar_prefetch=2,
            grid=(zs,),
            in_specs=[
                pl.BlockSpec((None, nrhs, size), lambda z, at, w: (at[0], 0, 0)),
                pl.BlockSpec((2 * leaves, size, size), lambda z, *_: (z, 0, 0)),
            ],
            out_specs=(spec, spec),
        ),
        name="back_products",
    )(jnp.stack([row, core]), pattern, solution, coupled)


def sum_over(value, axis, size):
    value = value.astype(BF)
    got = [value] + [
        lax.ppermute(value, axis, [(i, (i + k) % size) for i in range(size)])
        for k in range(1, size)
    ]
    got = [g.astype(F32) for g in got]
    return (got[0] + got[2]) + (got[1] + got[3])


def build(mesh):
    subs, zs, cores, cols = mesh.devices.shape

    def local(leaf_rhs, leaf_inverse, coupling, pattern, top_rhs, top_inverse, top_factor):
        core = lax.axis_index("core")
        col = lax.axis_index("col")
        row = lax.axis_index("z") * cores + core
        own_rhs = leaf_rhs[0, :, 0]
        own_inverse = jnp.tril(leaf_inverse[0, :, 0])
        coupled = coupling[0, 0, :, 0]
        weights = pattern[0, 0, :, 0].astype(BF)
        leaves, nrhs, size = own_rhs.shape
        rows = zs * cores
        assert top_factor.shape[1] == subs

        sub = lax.axis_index("sub")
        column = subs * col + sub
        block = lax.dynamic_index_in_dim(top_factor[0], sub, 0, keepdims=False)
        half = size // 2
        pairs = []
        for i in range(subs * rows * cols):
            s, rest = divmod(i, rows * cols)
            r, c = divmod(rest, cols)
            if r > subs * c + s:
                pairs.append((i, subs * rows * cols - 1 - i))
        moved = lax.ppermute(block[half:], ("sub", "z", "core", "col"), pairs)
        unit = jnp.where(row > column, block[:half], moved)
        ring = lax.all_to_all(
            jnp.broadcast_to(unit[None], (zs,) + unit.shape), "z", 0, 0, tiled=True
        )

        def units(a, b):
            c, s = divmod(b, subs)
            at = ((s * cols + c) * cores + a % cores) * zs + a // cores
            return at, subs * rows * cols - 1 - at

        top_tri = jnp.tril(top_inverse)

        leaf_forward = jnp.einsum(
            "inb,idb->ind", own_rhs, own_inverse, preferred_element_type=F32
        ).astype(BF)
        leaf_shared, ring = lax.optimization_barrier((leaf_forward, ring))
        factor = lax.all_gather(ring, ("sub", "col", "core"), axis=0, tiled=True)
        mine = lax.all_to_all(
            jnp.broadcast_to(leaf_shared[None], (zs,) + leaf_forward.shape),
            "z", 0, 0, tiled=True,
        )
        other = lax.ppermute(mine, "core", SWAP)
        first = core == 0
        forward = jnp.stack(
            [jnp.where(first, mine, other), jnp.where(first, other, mine)], axis=1
        ).reshape(rows * leaves, nrhs, size)
        partial = jnp.einsum(
            "inb,ieb->ne", forward * weights[:, None, None], coupled,
            preferred_element_type=F32,
        )
        update = sum_over(sum_over(partial, "sub", subs), "col", cols).astype(BF)
        updates = lax.all_gather(update, ROW, axis=0)

        solution = top_solve(units, top_rhs, updates, top_tri, factor)
        own_top = lax.dynamic_index_in_dim(solution, row, 0, keepdims=False)

        mine, other = back_products(
            solution, coupled, pattern[0, 0, :, 0], row, core, zs, leaves
        )
        other = lax.ppermute(other, "core", SWAP)
        pair = (mine.astype(F32) + other.astype(F32)).astype(BF)
        spread = lax.all_to_all(pair, "z", 0, 0, tiled=True)
        back_sums = jnp.sum(spread.astype(F32), axis=0)
        leaf_residue = (leaf_forward.astype(F32) - back_sums).astype(BF)
        leaf_result = jnp.einsum(
            "inb,ibd->ind", leaf_residue, own_inverse, preferred_element_type=F32
        ).astype(BF)
        return leaf_result[None, :, None], own_top[None]

    return local


def solution(mesh):
    subs, rows, cols = (mesh.shape[name] for name in ("sub", "row", "col"))
    mesh = Mesh(
        mesh.devices.reshape(subs, rows // 2, 2, cols), ("sub", "z", "core", "col")
    )
    placed = (
        P("sub", ROW, "col", None, None),
        P("sub", ROW, "col", None, None),
        P("sub", ROW, None, "col", None, None),
        P("sub", ROW, None, "col"),
        P(),
        P(),
        P(ROW, "col", None, None),
    )
    return jax.shard_map(
        build(mesh),
        mesh=mesh,
        in_specs=placed,
        out_specs=(P("sub", ROW, "col", None, None), P(ROW, None, None)),
        check_vma=False,
    )
```

```python
import jax
import jax.numpy as jnp
from jax import lax
from jax.experimental import pallas as pl
from jax.experimental.pallas import tpu as pltpu
from jax.sharding import Mesh, PartitionSpec as P

BF = jnp.bfloat16
F32 = jnp.float32
ROW = ("z", "core")
SWAP = [(0, 1), (1, 0)]
NT = (((1,), (1,)), ((), ()))
NN = (((1,), (0,)), ((), ()))


def first_block(a):
    return a * (a - 1) // 2


def top_kernel(
    units, at_ref, w_ref, r_ref, u_ref, g_ref, f_hbm, c_hbm,
    top_ref, mine_ref, other_ref, zs, xs, fac, coup, sems, coup_sem,
):
    count = r_ref.shape[0]
    half = f_hbm.shape[1]
    chips, leaves = mine_ref.shape[:2]

    def dot(a, b, dims):
        return lax.dot_general(a, b, dims, preferred_element_type=F32)

    def rhs(k):
        return r_ref[k].astype(F32) - u_ref[k].astype(F32)

    def block(a, b):
        return fac[first_block(a) + b]

    for a in range(1, count):
        for b in range(a):
            for part, unit in enumerate(units(a, b)):
                pltpu.make_async_copy(
                    f_hbm.at[unit],
                    fac.at[first_block(a) + b, pl.ds(part * half, half)],
                    sems.at[a],
                ).start()
    coupling = pltpu.make_async_copy(c_hbm, coup, coup_sem)
    coupling.start()

    summed = rhs(0)
    for k in range(count):
        z = dot(summed.astype(BF), g_ref[k], NT).astype(BF)
        zs[k] = z
        if k + 1 < count:
            row = fac.at[pl.ds(first_block(k + 1), k + 1)]
            pltpu.make_async_copy(row, row, sems.at[k + 1]).wait()
            later = rhs(k + 1)
            for b in range(k):
                later -= dot(zs[b], block(k + 1, b), NT)
            summed = later - dot(z, block(k + 1, k), NT)
    summed = zs[count - 1].astype(F32)
    for k in reversed(range(count)):
        x = dot(summed.astype(BF), g_ref[k], NN).astype(BF)
        xs[k] = x
        if k > 0:
            later = zs[k - 1].astype(F32)
            for a in range(count - 1, k, -1):
                later -= dot(xs[a], block(a, k - 1), NN)
            summed = later - dot(x, block(k, k - 1), NN)

    own = xs[at_ref[0]]
    top_ref[...] = own
    core = at_ref[1]
    coupling.wait()
    for out, part in ((other_ref, 1 - core), (mine_ref, core)):
        for chip in range(chips):
            for leaf in range(leaves):
                at = (2 * chip + part) * leaves + leaf
                weight = w_ref[at].astype(F32)
                out[chip, leaf] = (dot(own, coup[at], NN) * weight).astype(BF)


def top_solve(units, at, pattern, rhs, updates, inverse, factor, coupled, chips, leaves):
    whole = pl.BlockSpec(memory_space=pltpu.VMEM)
    scalars = pl.BlockSpec(memory_space=pltpu.SMEM)
    placed = pl.BlockSpec(memory_space=pltpu.HBM)
    count, nrhs, size = rhs.shape
    part = jax.ShapeDtypeStruct((chips, leaves, nrhs, size), BF)
    return pl.pallas_call(
        lambda *refs: top_kernel(units, *refs),
        out_shape=(jax.ShapeDtypeStruct((nrhs, size), BF), part, part),
        in_specs=[scalars] * 2 + [whole] * 3 + [placed] * 2,
        out_specs=(whole,) * 3,
        scratch_shapes=[
            pltpu.VMEM(rhs.shape, BF),
            pltpu.VMEM(rhs.shape, BF),
            pltpu.VMEM((first_block(count), size, size), BF),
            pltpu.VMEM(coupled.shape, BF),
            pltpu.SemaphoreType.DMA((count,)),
            pltpu.SemaphoreType.DMA,
        ],
        compiler_params=pltpu.CompilerParams(vmem_limit_bytes=40 << 20),
        name="top_solve",
    )(at, pattern, rhs, updates, inverse, factor, coupled)


def sum_over(value, axis, size):
    value = value.astype(BF)
    got = [value] + [
        lax.ppermute(value, axis, [(i, (i + k) % size) for i in range(size)])
        for k in range(1, size)
    ]
    got = [g.astype(F32) for g in got]
    return (got[0] + got[2]) + (got[1] + got[3])


def build(mesh):
    subs, zs, cores, cols = mesh.devices.shape

    def local(leaf_rhs, leaf_inverse, coupling, pattern, top_rhs, top_inverse, top_factor):
        core = lax.axis_index("core")
        col = lax.axis_index("col")
        row = lax.axis_index("z") * cores + core
        own_rhs = leaf_rhs[0, :, 0]
        own_inverse = jnp.tril(leaf_inverse[0, :, 0])
        coupled = coupling[0, 0, :, 0]
        weights = pattern[0, 0, :, 0].astype(BF)
        leaves, nrhs, size = own_rhs.shape
        rows = zs * cores
        assert top_factor.shape[1] == subs

        sub = lax.axis_index("sub")
        column = subs * col + sub
        block = lax.dynamic_index_in_dim(top_factor[0], sub, 0, keepdims=False)
        half = size // 2
        pairs = []
        for i in range(subs * rows * cols):
            s, rest = divmod(i, rows * cols)
            r, c = divmod(rest, cols)
            if r > subs * c + s:
                pairs.append((i, subs * rows * cols - 1 - i))
        moved = lax.ppermute(block[half:], ("sub", "z", "core", "col"), pairs)
        eight = (zs,) + moved.shape
        unit = jnp.where(
            row > column,
            jnp.broadcast_to(block[None, :half], eight),
            jnp.broadcast_to(moved[None], eight),
        )
        ring = lax.all_to_all(unit, "z", 0, 0, tiled=True)

        def units(a, b):
            c, s = divmod(b, subs)
            at = ((s * cols + c) * cores + a % cores) * zs + a // cores
            return at, subs * rows * cols - 1 - at

        top_tri = jnp.tril(top_inverse)

        leaf_forward = jnp.einsum(
            "inb,idb->ind", own_rhs, own_inverse, preferred_element_type=F32
        ).astype(BF)
        leaf_shared, ring = lax.optimization_barrier((leaf_forward, ring))
        factor = lax.all_gather(ring, ("sub", "col", "core"), axis=0, tiled=True)
        mine = lax.all_to_all(
            jnp.broadcast_to(leaf_shared[None], (zs,) + leaf_forward.shape),
            "z", 0, 0, tiled=True,
        )
        other = lax.ppermute(mine, "core", SWAP)
        first = core == 0
        forward = jnp.stack(
            [jnp.where(first, mine, other), jnp.where(first, other, mine)], axis=1
        ).reshape(rows * leaves, nrhs, size)
        partial = jnp.einsum(
            "inb,ieb->ne", forward * weights[:, None, None], coupled,
            preferred_element_type=F32,
        )
        update = sum_over(sum_over(partial, "sub", subs), "col", cols).astype(BF)
        updates = lax.all_gather(update, ROW, axis=0)

        own_top, mine, other = top_solve(
            units, jnp.stack([row, core]), pattern[0, 0, :, 0], top_rhs, updates,
            top_tri, factor, coupled, zs, leaves,
        )
        other = lax.ppermute(other, "core", SWAP)
        pair = (mine.astype(F32) + other.astype(F32)).astype(BF)
        spread = lax.all_to_all(pair, "z", 0, 0, tiled=True)
        back_sums = jnp.sum(spread.astype(F32), axis=0)
        leaf_residue = (leaf_forward.astype(F32) - back_sums).astype(BF)
        leaf_result = jnp.einsum(
            "inb,ibd->ind", leaf_residue, own_inverse, preferred_element_type=F32
        ).astype(BF)
        return leaf_result[None, :, None], own_top[None]

    return local


def solution(mesh):
    subs, rows, cols = (mesh.shape[name] for name in ("sub", "row", "col"))
    mesh = Mesh(
        mesh.devices.reshape(subs, rows // 2, 2, cols), ("sub", "z", "core", "col")
    )
    placed = (
        P("sub", ROW, "col", None, None),
        P("sub", ROW, "col", None, None),
        P("sub", ROW, None, "col", None, None),
        P("sub", ROW, None, "col"),
        P(),
        P(),
        P(ROW, "col", None, None),
    )
    return jax.shard_map(
        build(mesh),
        mesh=mesh,
        in_specs=placed,
        out_specs=(P("sub", ROW, "col", None, None), P(ROW, None, None)),
        check_vma=False,
    )
```

```python
import jax
import jax.numpy as jnp
from jax import lax
from jax.experimental import pallas as pl
from jax.experimental.pallas import tpu as pltpu
from jax.sharding import Mesh, PartitionSpec as P

BF = jnp.bfloat16
F32 = jnp.float32
ROW = ("z", "core")
SWAP = [(0, 1), (1, 0)]
NT = (((1,), (1,)), ((), ()))
NN = (((1,), (0,)), ((), ()))


def hop(size):
    return [
        (2 * z + core, 2 * ((z + 1 - 2 * core) % size) + core)
        for z in range(size)
        for core in range(2)
    ]


def update_kernel(count, base_ref, w_ref, *refs):
    parts, (c_hbm, out_ref, coup, sems) = refs[:-4], refs[-4:]
    leaves = coup.shape[1]

    def fetch(i):
        return pltpu.make_async_copy(
            c_hbm.at[pl.ds(base_ref[i], leaves)], coup.at[i], sems.at[i]
        )

    for i in range(count):
        fetch(i).start()
    total = None
    i = 0
    for part in parts:
        groups = [part] if len(part.shape) == 3 else [part.at[0], part.at[1]]
        for group in groups:
            fetch(i).wait()
            for leaf in range(leaves):
                weight = w_ref[base_ref[i] + leaf].astype(F32)
                term = weight * lax.dot_general(
                    group[leaf], coup[i, leaf], NT, preferred_element_type=F32
                )
                total = term if total is None else total + term
            i += 1
    out_ref[...] = total


def update_products(base, pattern, parts, coupled):
    count = sum(1 if part.ndim == 3 else 2 for part in parts)
    leaves, nrhs, size = parts[0].shape[-3:]
    whole = pl.BlockSpec(memory_space=pltpu.VMEM)
    scalars = pl.BlockSpec(memory_space=pltpu.SMEM)
    return pl.pallas_call(
        lambda *refs: update_kernel(count, *refs),
        out_shape=jax.ShapeDtypeStruct((nrhs, size), F32),
        in_specs=[scalars] * 2
        + [whole] * len(parts)
        + [pl.BlockSpec(memory_space=pltpu.HBM)],
        out_specs=whole,
        scratch_shapes=[
            pltpu.VMEM((count, leaves, size, size), BF),
            pltpu.SemaphoreType.DMA((count,)),
        ],
        compiler_params=pltpu.CompilerParams(vmem_limit_bytes=58 << 20),
        cost_estimate=pl.CostEstimate(
            flops=2 * count * leaves * nrhs * size * size,
            bytes_accessed=2 * count * leaves * size * (size + nrhs),
            transcendentals=0,
        ),
        name="update_products",
    )(base, pattern, *parts, coupled)


def first_block(a):
    return a * (a - 1) // 2


def top_kernel(
    units, at_ref, w_ref, r_ref, u_ref, g_ref, f_hbm, c_hbm,
    top_ref, mine_ref, other_ref, zs, xs, fac, coup, sems, coup_sem,
):
    count = r_ref.shape[0]
    half = f_hbm.shape[2]
    chips, leaves = mine_ref.shape[:2]

    def dot(a, b, dims):
        return lax.dot_general(a, b, dims, preferred_element_type=F32)

    def rhs(k):
        return r_ref[k].astype(F32) - u_ref[k].astype(F32)

    def block(a, b):
        return fac[first_block(a) + b]

    for a in range(1, count):
        for b in range(a):
            for part, (group, chip) in enumerate(units(a, b)):
                pltpu.make_async_copy(
                    f_hbm.at[group, chip],
                    fac.at[first_block(a) + b, pl.ds(part * half, half)],
                    sems.at[a],
                ).start()
    coupling = pltpu.make_async_copy(c_hbm, coup, coup_sem)
    coupling.start()

    summed = rhs(0)
    for k in range(count):
        z = dot(summed.astype(BF), g_ref[k], NT).astype(BF)
        zs[k] = z
        if k + 1 < count:
            row = fac.at[pl.ds(first_block(k + 1), k + 1)]
            pltpu.make_async_copy(row, row, sems.at[k + 1]).wait()
            later = rhs(k + 1)
            for b in range(k):
                later -= dot(zs[b], block(k + 1, b), NT)
            summed = later - dot(z, block(k + 1, k), NT)
    summed = zs[count - 1].astype(F32)
    for k in reversed(range(count)):
        x = dot(summed.astype(BF), g_ref[k], NN).astype(BF)
        xs[k] = x
        if k > 0:
            later = zs[k - 1].astype(F32)
            for a in range(count - 1, k, -1):
                later -= dot(xs[a], block(a, k - 1), NN)
            summed = later - dot(x, block(k, k - 1), NN)

    own = xs[at_ref[0]]
    top_ref[...] = own
    core = at_ref[1]
    coupling.wait()
    for out, part in ((other_ref, 1 - core), (mine_ref, core)):
        for chip in range(chips):
            for leaf in range(leaves):
                at = (2 * chip + part) * leaves + leaf
                weight = w_ref[at].astype(F32)
                out[chip, leaf] = (dot(own, coup[at], NN) * weight).astype(BF)


def top_solve(
    units, at, pattern, rhs, updates, inverse, factor, coupled, chips, leaves
):
    whole = pl.BlockSpec(memory_space=pltpu.VMEM)
    scalars = pl.BlockSpec(memory_space=pltpu.SMEM)
    placed = pl.BlockSpec(memory_space=pltpu.HBM)
    count, nrhs, size = rhs.shape
    part = jax.ShapeDtypeStruct((chips, leaves, nrhs, size), BF)
    return pl.pallas_call(
        lambda *refs: top_kernel(units, *refs),
        out_shape=(jax.ShapeDtypeStruct((nrhs, size), BF), part, part),
        in_specs=[scalars] * 2 + [whole] * 3 + [placed] * 2,
        out_specs=(whole,) * 3,
        scratch_shapes=[
            pltpu.VMEM(rhs.shape, BF),
            pltpu.VMEM(rhs.shape, BF),
            pltpu.VMEM((first_block(count), size, size), BF),
            pltpu.VMEM(coupled.shape, BF),
            pltpu.SemaphoreType.DMA((count,)),
            pltpu.SemaphoreType.DMA,
        ],
        compiler_params=pltpu.CompilerParams(vmem_limit_bytes=58 << 20),
        name="top_solve",
    )(at, pattern, rhs, updates, inverse, factor, coupled)


def sum_over(value, axis, size):
    value = value.astype(BF)
    got = [value] + [
        lax.ppermute(value, axis, [(i, (i + k) % size) for i in range(size)])
        for k in range(1, size)
    ]
    got = [g.astype(F32) for g in got]
    return (got[0] + got[2]) + (got[1] + got[3])


def build(mesh):
    subs, zs, cores, cols = mesh.devices.shape

    def local(leaf_rhs, leaf_inverse, coupling, pattern, top_rhs, top_inverse, top_factor):
        core = lax.axis_index("core")
        col = lax.axis_index("col")
        row = lax.axis_index("z") * cores + core
        own_rhs = leaf_rhs[0, :, 0]
        own_inverse = jnp.tril(leaf_inverse[0, :, 0])
        coupled = coupling[0, 0, :, 0]
        leaves, nrhs, size = own_rhs.shape
        rows = zs * cores
        assert top_factor.shape[1] == subs

        sub = lax.axis_index("sub")
        column = subs * col + sub
        block = lax.dynamic_index_in_dim(top_factor[0], sub, 0, keepdims=False)
        half = size // 2
        pairs = []
        for i in range(subs * rows * cols):
            s, rest = divmod(i, rows * cols)
            r, c = divmod(rest, cols)
            if r > subs * c + s:
                pairs.append((i, subs * rows * cols - 1 - i))
        moved = lax.ppermute(block[half:], ("sub", "z", "core", "col"), pairs)
        eight = (zs,) + moved.shape
        unit = jnp.where(
            row > column,
            jnp.broadcast_to(block[None, :half], eight),
            jnp.broadcast_to(moved[None], eight),
        )
        ring = lax.all_to_all(unit, "z", 0, 0, tiled=True)

        def units(a, b):
            c, s = divmod(b, subs)
            z, group_core = divmod(a, cores)
            group = (s * cols + c) * cores + group_core
            return (group, z), (subs * cols * cores - 1 - group, zs - 1 - z)

        top_tri = jnp.tril(top_inverse)
        present = pattern[0, 0, :, 0]

        leaf_forward = jnp.einsum(
            "inb,idb->ind", own_rhs, own_inverse, preferred_element_type=F32
        ).astype(BF)
        steps = hop(zs)
        swapped = lax.ppermute(leaf_forward, "core", SWAP)
        shard = jnp.stack([leaf_forward, swapped])
        early, late = [leaf_forward, swapped], []
        for step in range(1, zs // 2):
            shard = lax.ppermute(shard, ROW, steps)
            (late if step == zs // 2 - 1 else early).extend(
                [shard, lax.ppermute(shard, "core", SWAP)]
            )
        last = lax.ppermute(shard[0], ROW, steps)
        late.extend([last, lax.ppermute(last, "core", SWAP)])
        away = jnp.array(
            [0, 0]
            + [d for k in range(1, zs // 2) for d in (-k, -k, k, k)]
            + [zs // 2] * 2
        )
        flip = jnp.array([0, 1] + [0, 1, 1, 0] * (zs // 2 - 1) + [0, 1])
        chip = (lax.axis_index("z") + (1 - 2 * core) * away + zs) % zs
        part = jnp.where(flip == 1, 1 - core, core)
        base = ((chip * cores + part) * leaves).astype(jnp.int32)
        cut = sum(1 if part.ndim == 3 else 2 for part in early)

        ring, _ = lax.optimization_barrier((ring, shard))
        factor = lax.all_gather(ring, ("sub", "col", "core"), axis=0)

        partial = update_products(base[:cut], present, early, coupled)
        partial += update_products(base[cut:], present, late, coupled)
        update = sum_over(sum_over(partial, "sub", subs), "col", cols).astype(BF)
        updates = lax.all_gather(update, ROW, axis=0)

        own_top, mine, other = top_solve(
            units, jnp.stack([row, core]), present, top_rhs, updates,
            top_tri, factor, coupled, zs, leaves,
        )
        other = lax.ppermute(other, "core", SWAP)
        pair = (mine.astype(F32) + other.astype(F32)).astype(BF)
        spread = lax.all_to_all(pair, "z", 0, 0, tiled=True)
        back_sums = jnp.sum(spread.astype(F32), axis=0)
        leaf_residue = (leaf_forward.astype(F32) - back_sums).astype(BF)
        leaf_result = jnp.einsum(
            "inb,ibd->ind", leaf_residue, own_inverse, preferred_element_type=F32
        ).astype(BF)
        return leaf_result[None, :, None], own_top[None]

    return local


def solution(mesh):
    subs, rows, cols = (mesh.shape[name] for name in ("sub", "row", "col"))
    mesh = Mesh(
        mesh.devices.reshape(subs, rows // 2, 2, cols), ("sub", "z", "core", "col")
    )
    placed = (
        P("sub", ROW, "col", None, None),
        P("sub", ROW, "col", None, None),
        P("sub", ROW, None, "col", None, None),
        P("sub", ROW, None, "col"),
        P(),
        P(),
        P(ROW, "col", None, None),
    )
    return jax.shard_map(
        build(mesh),
        mesh=mesh,
        in_specs=placed,
        out_specs=(P("sub", ROW, "col", None, None), P(ROW, None, None)),
        check_vma=False,
    )
```

```python
import jax
import jax.numpy as jnp
from jax import lax
from jax.experimental import pallas as pl
from jax.experimental.pallas import tpu as pltpu
from jax.sharding import Mesh, PartitionSpec as P

BF = jnp.bfloat16
F32 = jnp.float32
ROW = ("z", "core")
SWAP = [(0, 1), (1, 0)]
NT = (((1,), (1,)), ((), ()))
NN = (((1,), (0,)), ((), ()))


def hop(size, far):
    return [
        (2 * z + core, 2 * ((z + far * (1 - 2 * core)) % size) + core)
        for z in range(size)
        for core in range(2)
    ]


def update_kernel(
    at_ref, w_ref, mine_ref, other_ref, c_hbm, out_ref, coup_ref, sems
):
    chips, leaves = mine_ref.shape[:2]
    per_chip = 2 * leaves
    core = at_ref[1]

    def fetch(chip):
        piece = pl.ds(chip * per_chip, per_chip)
        return pltpu.make_async_copy(
            c_hbm.at[piece], coup_ref.at[piece], sems.at[chip]
        )

    for chip in range(chips):
        fetch(chip).start()
    total = None
    for chip in range(chips):
        fetch(chip).wait()
        for rows, part in ((mine_ref, core), (other_ref, 1 - core)):
            for leaf in range(leaves):
                at = (2 * chip + part) * leaves + leaf
                weight = w_ref[at].astype(F32)
                term = weight * lax.dot_general(
                    rows[chip, leaf], coup_ref[at], NT, preferred_element_type=F32
                )
                total = term if total is None else total + term
    out_ref[...] = total


def update_products(at, pattern, mine, other, coupled):
    chips, leaves, nrhs, size = mine.shape
    whole = pl.BlockSpec(memory_space=pltpu.VMEM)
    scalars = pl.BlockSpec(memory_space=pltpu.SMEM)
    return pl.pallas_call(
        update_kernel,
        out_shape=jax.ShapeDtypeStruct((nrhs, size), F32),
        in_specs=[scalars] * 2
        + [whole] * 2
        + [pl.BlockSpec(memory_space=pltpu.HBM)],
        out_specs=whole,
        scratch_shapes=[
            pltpu.VMEM(coupled.shape, BF),
            pltpu.SemaphoreType.DMA((chips,)),
        ],
        compiler_params=pltpu.CompilerParams(vmem_limit_bytes=16 << 20),
        name="update_products",
    )(
        at, pattern, mine, other,
        pltpu.with_memory_space_constraint(coupled, pltpu.HBM),
    )


def first_block(a):
    return a * (a - 1) // 2


def group_fetches(base_ref, c_hbm, coup, sems):
    groups, leaves = coup.shape[:2]
    return [
        pltpu.make_async_copy(
            c_hbm.at[pl.ds(base_ref[i], leaves)], coup.at[i], sems.at[i]
        )
        for i in range(groups)
    ]


def group_products(own, base_ref, w_ref, fetch, coup, outs):
    leaves = coup.shape[1]
    i = 0
    for out in outs:
        for group in range(out.shape[0]):
            fetch[i].wait()
            for leaf in range(leaves):
                weight = w_ref[base_ref[i] + leaf].astype(F32)
                value = lax.dot_general(
                    own, coup[i, leaf], NN, preferred_element_type=F32
                )
                out[group, leaf] = (value * weight).astype(BF)
            i += 1


def near_kernel(base_ref, w_ref, own_ref, c_hbm, keep_ref, give_ref, coup, sems):
    fetch = group_fetches(base_ref, c_hbm, coup, sems)
    for copy in fetch:
        copy.start()
    group_products(
        own_ref[...], base_ref, w_ref, fetch, coup, (give_ref, keep_ref)
    )


def near_products(base, pattern, own, coupled, leaves):
    nrhs, size = own.shape
    groups = base.shape[0]
    whole = pl.BlockSpec(memory_space=pltpu.VMEM)
    scalars = pl.BlockSpec(memory_space=pltpu.SMEM)
    part = jax.ShapeDtypeStruct((groups // 2, leaves, nrhs, size), BF)
    return pl.pallas_call(
        near_kernel,
        out_shape=(part, part),
        in_specs=[scalars] * 2 + [whole, pl.BlockSpec(memory_space=pltpu.HBM)],
        out_specs=(whole,) * 2,
        scratch_shapes=[
            pltpu.VMEM((groups, leaves, size, size), BF),
            pltpu.SemaphoreType.DMA((groups,)),
        ],
        compiler_params=pltpu.CompilerParams(vmem_limit_bytes=16 << 20),
        cost_estimate=pl.CostEstimate(
            flops=2 * groups * leaves * nrhs * size * size,
            bytes_accessed=2 * groups * leaves * size * (size + nrhs),
            transcendentals=0,
        ),
        name="near_products",
    )(base, pattern, own, pltpu.with_memory_space_constraint(coupled, pltpu.HBM))


def top_kernel(
    units, at_ref, base_ref, w_ref, r_ref, u_ref, g_ref, f_hbm, c_hbm,
    top_ref, keep_ref, give_ref, zs, xs, fac, coup, sems, coup_sems,
):
    count = r_ref.shape[0]
    half = f_hbm.shape[1]

    def dot(a, b, dims):
        return lax.dot_general(a, b, dims, preferred_element_type=F32)

    def rhs(k):
        return r_ref[k].astype(F32) - u_ref[k].astype(F32)

    def block(a, b):
        return fac[first_block(a) + b]

    for a in range(1, count):
        for b in range(a):
            for part, unit in enumerate(units(a, b)):
                pltpu.make_async_copy(
                    f_hbm.at[unit],
                    fac.at[first_block(a) + b, pl.ds(part * half, half)],
                    sems.at[a],
                ).start()

    summed = rhs(0)
    for k in range(count):
        z = dot(summed.astype(BF), g_ref[k], NT).astype(BF)
        zs[k] = z
        if k + 1 < count:
            row = fac.at[pl.ds(first_block(k + 1), k + 1)]
            pltpu.make_async_copy(row, row, sems.at[k + 1]).wait()
            later = rhs(k + 1)
            for b in range(k):
                later -= dot(zs[b], block(k + 1, b), NT)
            summed = later - dot(z, block(k + 1, k), NT)
    fetch = group_fetches(base_ref, c_hbm, coup, coup_sems)
    for copy in fetch:
        copy.start()
    summed = zs[count - 1].astype(F32)
    for k in reversed(range(count)):
        x = dot(summed.astype(BF), g_ref[k], NN).astype(BF)
        xs[k] = x
        if k > 0:
            later = zs[k - 1].astype(F32)
            for a in range(count - 1, k, -1):
                later -= dot(xs[a], block(a, k - 1), NN)
            summed = later - dot(x, block(k, k - 1), NN)

    own = xs[at_ref[0]]
    top_ref[...] = own
    group_products(own, base_ref, w_ref, fetch, coup, (give_ref, keep_ref))


def top_solve(units, at, base, pattern, rhs, updates, inverse, factor, coupled, leaves):
    whole = pl.BlockSpec(memory_space=pltpu.VMEM)
    scalars = pl.BlockSpec(memory_space=pltpu.SMEM)
    count, nrhs, size = rhs.shape
    groups = base.shape[0]
    part = jax.ShapeDtypeStruct((groups // 2, leaves, nrhs, size), BF)
    return pl.pallas_call(
        lambda *refs: top_kernel(units, *refs),
        out_shape=(jax.ShapeDtypeStruct((nrhs, size), BF), part, part),
        in_specs=[scalars] * 3
        + [whole] * 3
        + [pl.BlockSpec(memory_space=pltpu.HBM)] * 2,
        out_specs=(whole,) * 3,
        scratch_shapes=[
            pltpu.VMEM(rhs.shape, BF),
            pltpu.VMEM(rhs.shape, BF),
            pltpu.VMEM((first_block(count), size, size), BF),
            pltpu.VMEM((groups, leaves, size, size), BF),
            pltpu.SemaphoreType.DMA((count,)),
            pltpu.SemaphoreType.DMA((groups,)),
        ],
        compiler_params=pltpu.CompilerParams(vmem_limit_bytes=32 << 20),
        name="top_solve",
    )(
        at, base, pattern, rhs, updates, inverse,
        pltpu.with_memory_space_constraint(factor, pltpu.HBM),
        pltpu.with_memory_space_constraint(coupled, pltpu.HBM),
    )


def sum_over(value, axis, size):
    value = value.astype(BF)
    got = [value] + [
        lax.ppermute(value, axis, [(i, (i + k) % size) for i in range(size)])
        for k in range(1, size)
    ]
    got = [g.astype(F32) for g in got]
    return (got[0] + got[2]) + (got[1] + got[3])


def build(mesh):
    subs, zs, cores, cols = mesh.devices.shape

    def local(leaf_rhs, leaf_inverse, coupling, pattern, top_rhs, top_inverse, top_factor):
        core = lax.axis_index("core")
        col = lax.axis_index("col")
        row = lax.axis_index("z") * cores + core
        own_rhs = leaf_rhs[0, :, 0]
        own_inverse = jnp.tril(leaf_inverse[0, :, 0])
        coupled = coupling[0, 0, :, 0]
        leaves, nrhs, size = own_rhs.shape
        rows = zs * cores
        assert top_factor.shape[1] == subs

        sub = lax.axis_index("sub")
        column = subs * col + sub
        block = lax.dynamic_index_in_dim(top_factor[0], sub, 0, keepdims=False)
        half = size // 2
        pairs = []
        for i in range(subs * rows * cols):
            s, rest = divmod(i, rows * cols)
            r, c = divmod(rest, cols)
            if r > subs * c + s:
                pairs.append((i, subs * rows * cols - 1 - i))
        moved = lax.ppermute(block[half:], ("sub", "z", "core", "col"), pairs)
        eight = (zs,) + moved.shape
        unit = jnp.where(
            row > column,
            jnp.broadcast_to(block[None, :half], eight),
            jnp.broadcast_to(moved[None], eight),
        )
        ring = lax.all_to_all(unit, "z", 0, 0, tiled=True)

        def units(a, b):
            c, s = divmod(b, subs)
            at = ((s * cols + c) * cores + a % cores) * zs + a // cores
            return at, subs * rows * cols - 1 - at

        top_tri = jnp.tril(top_inverse)

        leaf_forward = jnp.einsum(
            "inb,idb->ind", own_rhs, own_inverse, preferred_element_type=F32
        ).astype(BF)
        leaf_shared, ring = lax.optimization_barrier((leaf_forward, ring))
        factor = lax.all_gather(ring, ("sub", "col", "core"), axis=0, tiled=True)
        mine = lax.all_to_all(
            jnp.broadcast_to(leaf_shared[None], (zs,) + leaf_forward.shape),
            "z", 0, 0, tiled=True,
        )
        other = lax.ppermute(mine, "core", SWAP)
        at = jnp.stack([row, core])
        present = pattern[0, 0, :, 0]
        partial = update_products(at, present, mine, other, coupled)
        update = sum_over(sum_over(partial, "sub", subs), "col", cols).astype(BF)
        updates = lax.all_gather(update, ROW, axis=0)

        chip = lax.axis_index("z")
        turn = 1 - 2 * core
        other_core = 1 - core

        def base(groups):
            starts = [
                ((chip + away * turn + zs) % zs * cores + part) * leaves
                for away, part in groups
            ]
            return jnp.stack(starts).astype(jnp.int32)

        far_base = base(
            [(-3, 0), (-3, 1), (4, other_core), (3, 0), (3, 1), (4, core)]
        )
        near_base = base(
            [(-1, 0), (-1, 1), (-2, 0), (-2, 1), (0, other_core)]
            + [(1, 0), (1, 1), (2, 0), (2, 1), (0, core)]
        )

        own_top, keep, give = top_solve(
            units, at, far_base, present, top_rhs, updates, top_tri, factor,
            coupled, leaves,
        )
        got = lax.ppermute(give, "core", SWAP)
        sent = (keep.astype(F32) + got.astype(F32)).astype(BF)
        own_late, sent = lax.optimization_barrier((own_top, sent))
        passed = lax.ppermute(sent, ROW, hop(zs, 2)).astype(F32)
        keep, give = near_products(near_base, present, own_late, coupled, leaves)
        near = [
            keep[i:j].astype(F32) + lax.ppermute(give[i:j], "core", SWAP).astype(F32)
            for i, j in ((0, 2), (2, 4), (4, 5))
        ]
        upper = jnp.arange(cores)[:, None, None, None] == core
        one = (near[0] + passed[0:2]).astype(BF)
        two = (near[1] + jnp.where(upper, passed[2][None], 0.0)).astype(BF)
        arrived = lax.ppermute(one, ROW, hop(zs, 1)).astype(F32) + lax.ppermute(
            two, ROW, hop(zs, 2)
        ).astype(F32)
        first = core == 0
        rest = jnp.where(first, arrived[1], arrived[0]).astype(BF)
        rest = lax.ppermute(rest, "core", SWAP).astype(F32)
        back_sums = near[2][0] + jnp.where(first, arrived[0], arrived[1]) + rest
        leaf_residue = (leaf_forward.astype(F32) - back_sums).astype(BF)
        leaf_result = jnp.einsum(
            "inb,ibd->ind", leaf_residue, own_inverse, preferred_element_type=F32
        ).astype(BF)
        return leaf_result[None, :, None], own_top[None]

    return local


def solution(mesh):
    subs, rows, cols = (mesh.shape[name] for name in ("sub", "row", "col"))
    mesh = Mesh(
        mesh.devices.reshape(subs, rows // 2, 2, cols), ("sub", "z", "core", "col")
    )
    placed = (
        P("sub", ROW, "col", None, None),
        P("sub", ROW, "col", None, None),
        P("sub", ROW, None, "col", None, None),
        P("sub", ROW, None, "col"),
        P(),
        P(),
        P(ROW, "col", None, None),
    )
    return jax.shard_map(
        build(mesh),
        mesh=mesh,
        in_specs=placed,
        out_specs=(P("sub", ROW, "col", None, None), P(ROW, None, None)),
        check_vma=False,
    )
```

```python
import jax
import jax.numpy as jnp
from jax import lax
from jax.experimental import pallas as pl
from jax.experimental.pallas import tpu as pltpu
from jax.sharding import Mesh, PartitionSpec as P

BF = jnp.bfloat16
F32 = jnp.float32
ROW = ("z", "core")
SWAP = [(0, 1), (1, 0)]
NT = (((1,), (1,)), ((), ()))
NN = (((1,), (0,)), ((), ()))


def hop(size, far):
    return [
        (2 * z + core, 2 * ((z + far * (1 - 2 * core)) % size) + core)
        for z in range(size)
        for core in range(2)
    ]


def update_kernel(base_ref, w_ref, *refs):
    parts, (c_hbm, out_ref, coup, sems) = refs[:-4], refs[-4:]
    fetch = group_fetches(base_ref, c_hbm, coup, sems)
    for copy in fetch:
        copy.start()
    total = None
    i = 0
    for part in parts:
        for group in range(part.shape[0]):
            fetch[i].wait()
            for leaf in range(coup.shape[1]):
                weight = w_ref[base_ref[i] + leaf].astype(F32)
                term = weight * lax.dot_general(
                    part[group, leaf], coup[i, leaf], NT, preferred_element_type=F32
                )
                total = term if total is None else total + term
            i += 1
    out_ref[...] = total


def update_products(base, pattern, parts, coupled):
    groups = base.shape[0]
    leaves, nrhs, size = parts[0].shape[1:]
    whole = pl.BlockSpec(memory_space=pltpu.VMEM)
    scalars = pl.BlockSpec(memory_space=pltpu.SMEM)
    return pl.pallas_call(
        update_kernel,
        out_shape=jax.ShapeDtypeStruct((nrhs, size), F32),
        in_specs=[scalars] * 2
        + [whole] * len(parts)
        + [pl.BlockSpec(memory_space=pltpu.HBM)],
        out_specs=whole,
        scratch_shapes=[
            pltpu.VMEM((groups, leaves, size, size), BF),
            pltpu.SemaphoreType.DMA((groups,)),
        ],
        compiler_params=pltpu.CompilerParams(vmem_limit_bytes=16 << 20),
        cost_estimate=pl.CostEstimate(
            flops=2 * groups * leaves * nrhs * size * size,
            bytes_accessed=2 * groups * leaves * size * (size + nrhs),
            transcendentals=0,
        ),
        name="update_products",
    )(
        base, pattern, *parts,
        pltpu.with_memory_space_constraint(coupled, pltpu.HBM),
    )


def first_block(a):
    return a * (a - 1) // 2


def group_fetches(base_ref, c_hbm, coup, sems):
    groups, leaves = coup.shape[:2]
    return [
        pltpu.make_async_copy(
            c_hbm.at[pl.ds(base_ref[i], leaves)], coup.at[i], sems.at[i]
        )
        for i in range(groups)
    ]


def group_products(own, base_ref, w_ref, fetch, coup, outs):
    leaves = coup.shape[1]
    for copy in fetch:
        copy.wait()
    i = 0
    for out in outs:
        for group in range(out.shape[0]):
            for leaf in range(leaves):
                weight = w_ref[base_ref[i] + leaf].astype(F32)
                value = lax.dot_general(
                    own, coup[i, leaf], NN, preferred_element_type=F32
                )
                out[group, leaf] = (value * weight).astype(BF)
            i += 1


def near_kernel(base_ref, w_ref, own_ref, c_hbm, keep_ref, give_ref, coup, sems):
    fetch = group_fetches(base_ref, c_hbm, coup, sems)
    for copy in fetch:
        copy.start()
    group_products(
        own_ref[...], base_ref, w_ref, fetch, coup, (give_ref, keep_ref)
    )


def near_products(base, pattern, own, coupled, leaves):
    nrhs, size = own.shape
    groups = base.shape[0]
    whole = pl.BlockSpec(memory_space=pltpu.VMEM)
    scalars = pl.BlockSpec(memory_space=pltpu.SMEM)
    part = jax.ShapeDtypeStruct((groups // 2, leaves, nrhs, size), BF)
    return pl.pallas_call(
        near_kernel,
        out_shape=(part, part),
        in_specs=[scalars] * 2 + [whole, pl.BlockSpec(memory_space=pltpu.HBM)],
        out_specs=(whole,) * 2,
        scratch_shapes=[
            pltpu.VMEM((groups, leaves, size, size), BF),
            pltpu.SemaphoreType.DMA((groups,)),
        ],
        compiler_params=pltpu.CompilerParams(vmem_limit_bytes=16 << 20),
        cost_estimate=pl.CostEstimate(
            flops=2 * groups * leaves * nrhs * size * size,
            bytes_accessed=2 * groups * leaves * size * (size + nrhs),
            transcendentals=0,
        ),
        name="near_products",
    )(base, pattern, own, pltpu.with_memory_space_constraint(coupled, pltpu.HBM))


def top_kernel(
    units, at_ref, base_ref, w_ref, r_ref, u_ref, g_ref, f_hbm, c_hbm,
    top_ref, keep_ref, give_ref, zs, xs, fac, coup, sems, coup_sems,
):
    count = r_ref.shape[0]
    half = f_hbm.shape[1]

    def dot(a, b, dims):
        return lax.dot_general(a, b, dims, preferred_element_type=F32)

    def rhs(k):
        return r_ref[k].astype(F32) - u_ref[k].astype(F32)

    def block(a, b):
        return fac[first_block(a) + b]

    for a in range(1, count):
        for b in range(a):
            for part, unit in enumerate(units(a, b)):
                pltpu.make_async_copy(
                    f_hbm.at[unit],
                    fac.at[first_block(a) + b, pl.ds(part * half, half)],
                    sems.at[a],
                ).start()
    fetch = group_fetches(base_ref, c_hbm, coup, coup_sems)
    for copy in fetch:
        copy.start()

    summed = rhs(0)
    for k in range(count):
        z = dot(summed.astype(BF), g_ref[k], NT).astype(BF)
        zs[k] = z
        if k + 1 < count:
            row = fac.at[pl.ds(first_block(k + 1), k + 1)]
            pltpu.make_async_copy(row, row, sems.at[k + 1]).wait()
            later = rhs(k + 1)
            for b in range(k):
                later -= dot(zs[b], block(k + 1, b), NT)
            summed = later - dot(z, block(k + 1, k), NT)
    summed = zs[count - 1].astype(F32)
    for k in reversed(range(count)):
        x = dot(summed.astype(BF), g_ref[k], NN).astype(BF)
        xs[k] = x
        if k > 0:
            later = zs[k - 1].astype(F32)
            for a in range(count - 1, k, -1):
                later -= dot(xs[a], block(a, k - 1), NN)
            summed = later - dot(x, block(k, k - 1), NN)

    own = xs[at_ref[0]]
    top_ref[...] = own
    group_products(own, base_ref, w_ref, fetch, coup, (give_ref, keep_ref))


def top_solve(units, at, base, pattern, rhs, updates, inverse, factor, coupled, leaves):
    whole = pl.BlockSpec(memory_space=pltpu.VMEM)
    scalars = pl.BlockSpec(memory_space=pltpu.SMEM)
    count, nrhs, size = rhs.shape
    groups = base.shape[0]
    part = jax.ShapeDtypeStruct((groups // 2, leaves, nrhs, size), BF)
    return pl.pallas_call(
        lambda *refs: top_kernel(units, *refs),
        out_shape=(jax.ShapeDtypeStruct((nrhs, size), BF), part, part),
        in_specs=[scalars] * 3
        + [whole] * 3
        + [pl.BlockSpec(memory_space=pltpu.HBM)] * 2,
        out_specs=(whole,) * 3,
        scratch_shapes=[
            pltpu.VMEM(rhs.shape, BF),
            pltpu.VMEM(rhs.shape, BF),
            pltpu.VMEM((first_block(count), size, size), BF),
            pltpu.VMEM((groups, leaves, size, size), BF),
            pltpu.SemaphoreType.DMA((count,)),
            pltpu.SemaphoreType.DMA((groups,)),
        ],
        compiler_params=pltpu.CompilerParams(vmem_limit_bytes=32 << 20),
        name="top_solve",
    )(
        at, base, pattern, rhs, updates, inverse,
        pltpu.with_memory_space_constraint(factor, pltpu.HBM),
        pltpu.with_memory_space_constraint(coupled, pltpu.HBM),
    )


def sum_over(value, axis, size):
    value = value.astype(BF)
    got = [value] + [
        lax.ppermute(value, axis, [(i, (i + k) % size) for i in range(size)])
        for k in range(1, size)
    ]
    got = [g.astype(F32) for g in got]
    return (got[0] + got[2]) + (got[1] + got[3])


def build(mesh):
    subs, zs, cores, cols = mesh.devices.shape

    def local(leaf_rhs, leaf_inverse, coupling, pattern, top_rhs, top_inverse, top_factor):
        core = lax.axis_index("core")
        col = lax.axis_index("col")
        row = lax.axis_index("z") * cores + core
        own_rhs = leaf_rhs[0, :, 0]
        own_inverse = jnp.tril(leaf_inverse[0, :, 0])
        coupled = coupling[0, 0, :, 0]
        leaves, nrhs, size = own_rhs.shape
        rows = zs * cores
        assert top_factor.shape[1] == subs

        sub = lax.axis_index("sub")
        column = subs * col + sub
        block = lax.dynamic_index_in_dim(top_factor[0], sub, 0, keepdims=False)
        half = size // 2
        pairs = []
        for i in range(subs * rows * cols):
            s, rest = divmod(i, rows * cols)
            r, c = divmod(rest, cols)
            if r > subs * c + s:
                pairs.append((i, subs * rows * cols - 1 - i))
        moved = lax.ppermute(block[half:], ("sub", "z", "core", "col"), pairs)
        eight = (zs,) + moved.shape
        unit = jnp.where(
            row > column,
            jnp.broadcast_to(block[None, :half], eight),
            jnp.broadcast_to(moved[None], eight),
        )
        ring = lax.all_to_all(unit, "z", 0, 0, tiled=True)

        def units(a, b):
            c, s = divmod(b, subs)
            at = ((s * cols + c) * cores + a % cores) * zs + a // cores
            return at, subs * rows * cols - 1 - at

        top_tri = jnp.tril(top_inverse)

        leaf_forward = jnp.einsum(
            "inb,idb->ind", own_rhs, own_inverse, preferred_element_type=F32
        ).astype(BF)
        swapped = lax.ppermute(leaf_forward, "core", SWAP)
        shared, ring = lax.optimization_barrier(
            (jnp.stack([leaf_forward, swapped]), ring)
        )
        ring = pltpu.with_memory_space_constraint(ring, pltpu.HBM)
        factor = lax.all_gather(ring, ("sub", "col", "core"), axis=0, tiled=True)
        chip = lax.axis_index("z")
        turn = 1 - 2 * core
        other_core = 1 - core

        def base(groups):
            starts = [
                ((chip + away * turn + zs) % zs * cores + part) * leaves
                for away, part in groups
            ]
            return jnp.stack(starts).astype(jnp.int32)

        at = jnp.stack([row, core])
        present = pattern[0, 0, :, 0]
        one = lax.ppermute(shared, ROW, hop(zs, 1))
        two = lax.ppermute(shared, ROW, hop(zs, 2))
        far = lax.ppermute(jnp.concatenate([one, two[:1]]), ROW, hop(zs, 2))
        early = [shared, one, two] + [
            lax.ppermute(part, "core", SWAP) for part in (one, two)
        ]
        late = [far] + [
            lax.ppermute(part, "core", SWAP) for part in (far[:2], far[2:])
        ]
        own, opp = core, other_core
        early_base = base(
            [(0, own), (0, opp), (-1, own), (-1, opp), (-2, own), (-2, opp)]
            + [(1, opp), (1, own), (2, opp), (2, own)]
        )
        late_base = base(
            [(-3, own), (-3, opp), (4, own), (3, opp), (3, own), (4, opp)]
        )
        partial = update_products(early_base, present, early, coupled)
        partial += update_products(late_base, present, late, coupled)
        update = sum_over(sum_over(partial, "sub", subs), "col", cols).astype(BF)
        updates = lax.all_gather(update, ROW, axis=0)

        far_base = base(
            [(-3, 0), (-3, 1), (4, other_core), (3, 0), (3, 1), (4, core)]
        )
        near_base = base(
            [(-1, 0), (-1, 1), (-2, 0), (-2, 1), (0, other_core)]
            + [(1, 0), (1, 1), (2, 0), (2, 1), (0, core)]
        )

        own_top, keep, give = top_solve(
            units, at, far_base, present, top_rhs, updates, top_tri, factor,
            coupled, leaves,
        )
        got = lax.ppermute(give, "core", SWAP)
        sent = (keep.astype(F32) + got.astype(F32)).astype(BF)
        own_late, sent = lax.optimization_barrier((own_top, sent))
        passed = lax.ppermute(sent, ROW, hop(zs, 2)).astype(F32)
        keep, give = near_products(near_base, present, own_late, coupled, leaves)
        near = [
            keep[i:j].astype(F32) + lax.ppermute(give[i:j], "core", SWAP).astype(F32)
            for i, j in ((0, 2), (2, 4), (4, 5))
        ]
        upper = jnp.arange(cores)[:, None, None, None] == core
        one = (near[0] + passed[0:2]).astype(BF)
        two = (near[1] + jnp.where(upper, passed[2][None], 0.0)).astype(BF)
        arrived = lax.ppermute(one, ROW, hop(zs, 1)).astype(F32) + lax.ppermute(
            two, ROW, hop(zs, 2)
        ).astype(F32)
        first = core == 0
        rest = jnp.where(first, arrived[1], arrived[0]).astype(BF)
        rest = lax.ppermute(rest, "core", SWAP).astype(F32)
        back_sums = near[2][0] + jnp.where(first, arrived[0], arrived[1]) + rest
        leaf_residue = (leaf_forward.astype(F32) - back_sums).astype(BF)
        leaf_result = jnp.einsum(
            "inb,ibd->ind", leaf_residue, own_inverse, preferred_element_type=F32
        ).astype(BF)
        return leaf_result[None, :, None], own_top[None]

    return local


def solution(mesh):
    subs, rows, cols = (mesh.shape[name] for name in ("sub", "row", "col"))
    mesh = Mesh(
        mesh.devices.reshape(subs, rows // 2, 2, cols), ("sub", "z", "core", "col")
    )
    placed = (
        P("sub", ROW, "col", None, None),
        P("sub", ROW, "col", None, None),
        P("sub", ROW, None, "col", None, None),
        P("sub", ROW, None, "col"),
        P(),
        P(),
        P(ROW, "col", None, None),
    )
    return jax.shard_map(
        build(mesh),
        mesh=mesh,
        in_specs=placed,
        out_specs=(P("sub", ROW, "col", None, None), P(ROW, None, None)),
        check_vma=False,
    )
```

```python
import jax
import jax.numpy as jnp
from jax import lax
from jax.experimental import pallas as pl
from jax.experimental.pallas import tpu as pltpu
from jax.sharding import Mesh, PartitionSpec as P

BF = jnp.bfloat16
F32 = jnp.float32
ROW = ("z", "core")
SWAP = [(0, 1), (1, 0)]
NT = (((1,), (1,)), ((), ()))
NN = (((1,), (0,)), ((), ()))


def hop(size, far):
    return [
        (2 * z + core, 2 * ((z + far * (1 - 2 * core)) % size) + core)
        for z in range(size)
        for core in range(2)
    ]


def update_kernel(base_ref, w_ref, *refs):
    parts, (c_hbm, out_ref, coup, sems) = refs[:-4], refs[-4:]
    fetch = group_fetches(base_ref, c_hbm, coup, sems)
    for copy in fetch:
        copy.start()
    total = None
    i = 0
    for part in parts:
        for group in range(part.shape[0]):
            fetch[i].wait()
            for leaf in range(coup.shape[1]):
                weight = w_ref[base_ref[i] + leaf].astype(F32)
                term = weight * lax.dot_general(
                    part[group, leaf], coup[i, leaf], NT, preferred_element_type=F32
                )
                total = term if total is None else total + term
            i += 1
    out_ref[...] = total


def update_products(base, pattern, parts, coupled):
    groups = base.shape[0]
    leaves, nrhs, size = parts[0].shape[1:]
    whole = pl.BlockSpec(memory_space=pltpu.VMEM)
    scalars = pl.BlockSpec(memory_space=pltpu.SMEM)
    return pl.pallas_call(
        update_kernel,
        out_shape=jax.ShapeDtypeStruct((nrhs, size), F32),
        in_specs=[scalars] * 2
        + [whole] * len(parts)
        + [pl.BlockSpec(memory_space=pltpu.HBM)],
        out_specs=whole,
        scratch_shapes=[
            pltpu.VMEM((groups, leaves, size, size), BF),
            pltpu.SemaphoreType.DMA((groups,)),
        ],
        compiler_params=pltpu.CompilerParams(vmem_limit_bytes=16 << 20),
        cost_estimate=pl.CostEstimate(
            flops=2 * groups * leaves * nrhs * size * size,
            bytes_accessed=2 * groups * leaves * size * (size + nrhs),
            transcendentals=0,
        ),
        name="update_products",
    )(
        base, pattern, *parts,
        pltpu.with_memory_space_constraint(coupled, pltpu.HBM),
    )


def unit_kernel(held_ref, own_ref, moved_ref, out_ref):
    for held, source in ((1, own_ref), (0, moved_ref)):
        @pl.when(held_ref[0] == held)
        def _():
            for z in range(out_ref.shape[0]):
                out_ref[z] = source[...]


def spread_unit(held, own, moved, zs):
    whole = pl.BlockSpec(memory_space=pltpu.VMEM)
    return pl.pallas_call(
        unit_kernel,
        out_shape=jax.ShapeDtypeStruct((zs,) + own.shape, BF),
        in_specs=[pl.BlockSpec(memory_space=pltpu.SMEM), whole, whole],
        out_specs=whole,
        compiler_params=pltpu.CompilerParams(vmem_limit_bytes=4 << 20),
        name="spread_unit",
    )(held.astype(jnp.int32).reshape(1), own, moved)


def first_block(a):
    return a * (a - 1) // 2


def group_fetches(base_ref, c_hbm, coup, sems):
    groups, leaves = coup.shape[:2]
    return [
        pltpu.make_async_copy(
            c_hbm.at[pl.ds(base_ref[i], leaves)], coup.at[i], sems.at[i]
        )
        for i in range(groups)
    ]


def group_products(own, base_ref, w_ref, fetch, coup, outs):
    leaves = coup.shape[1]
    for copy in fetch:
        copy.wait()
    i = 0
    for out in outs:
        for group in range(out.shape[0]):
            for leaf in range(leaves):
                weight = w_ref[base_ref[i] + leaf].astype(F32)
                value = lax.dot_general(
                    own, coup[i, leaf], NN, preferred_element_type=F32
                )
                out[group, leaf] = (value * weight).astype(BF)
            i += 1


def near_kernel(base_ref, w_ref, own_ref, c_hbm, keep_ref, give_ref, coup, sems):
    fetch = group_fetches(base_ref, c_hbm, coup, sems)
    for copy in fetch:
        copy.start()
    group_products(
        own_ref[...], base_ref, w_ref, fetch, coup, (give_ref, keep_ref)
    )


def near_products(base, pattern, own, coupled, leaves):
    nrhs, size = own.shape
    groups = base.shape[0]
    whole = pl.BlockSpec(memory_space=pltpu.VMEM)
    scalars = pl.BlockSpec(memory_space=pltpu.SMEM)
    part = jax.ShapeDtypeStruct((groups // 2, leaves, nrhs, size), BF)
    return pl.pallas_call(
        near_kernel,
        out_shape=(part, part),
        in_specs=[scalars] * 2 + [whole, pl.BlockSpec(memory_space=pltpu.HBM)],
        out_specs=(whole,) * 2,
        scratch_shapes=[
            pltpu.VMEM((groups, leaves, size, size), BF),
            pltpu.SemaphoreType.DMA((groups,)),
        ],
        compiler_params=pltpu.CompilerParams(vmem_limit_bytes=16 << 20),
        cost_estimate=pl.CostEstimate(
            flops=2 * groups * leaves * nrhs * size * size,
            bytes_accessed=2 * groups * leaves * size * (size + nrhs),
            transcendentals=0,
        ),
        name="near_products",
    )(base, pattern, own, pltpu.with_memory_space_constraint(coupled, pltpu.HBM))


def top_kernel(
    units, at_ref, base_ref, w_ref, r_ref, u_ref, g_ref, f_hbm, c_hbm,
    top_ref, keep_ref, give_ref, zs, xs, fac, coup, sems, coup_sems,
):
    count = r_ref.shape[0]
    half = f_hbm.shape[1]

    def dot(a, b, dims):
        return lax.dot_general(a, b, dims, preferred_element_type=F32)

    def rhs(k):
        return r_ref[k].astype(F32) - u_ref[k].astype(F32)

    def block(a, b):
        return fac[first_block(a) + b]

    for a in range(1, count):
        for b in range(a):
            for part, unit in enumerate(units(a, b)):
                pltpu.make_async_copy(
                    f_hbm.at[unit],
                    fac.at[first_block(a) + b, pl.ds(part * half, half)],
                    sems.at[a],
                ).start()
    fetch = group_fetches(base_ref, c_hbm, coup, coup_sems)
    for copy in fetch:
        copy.start()

    summed = rhs(0)
    for k in range(count):
        z = dot(summed.astype(BF), g_ref[k], NT).astype(BF)
        zs[k] = z
        if k + 1 < count:
            row = fac.at[pl.ds(first_block(k + 1), k + 1)]
            pltpu.make_async_copy(row, row, sems.at[k + 1]).wait()
            later = rhs(k + 1)
            for b in range(k):
                later -= dot(zs[b], block(k + 1, b), NT)
            summed = later - dot(z, block(k + 1, k), NT)
    summed = zs[count - 1].astype(F32)
    for k in reversed(range(count)):
        x = dot(summed.astype(BF), g_ref[k], NN).astype(BF)
        xs[k] = x
        if k > 0:
            later = zs[k - 1].astype(F32)
            for a in range(count - 1, k, -1):
                later -= dot(xs[a], block(a, k - 1), NN)
            summed = later - dot(x, block(k, k - 1), NN)

    own = xs[at_ref[0]]
    top_ref[...] = own
    group_products(own, base_ref, w_ref, fetch, coup, (give_ref, keep_ref))


def top_solve(units, at, base, pattern, rhs, updates, inverse, factor, coupled, leaves):
    whole = pl.BlockSpec(memory_space=pltpu.VMEM)
    scalars = pl.BlockSpec(memory_space=pltpu.SMEM)
    count, nrhs, size = rhs.shape
    groups = base.shape[0]
    part = jax.ShapeDtypeStruct((groups // 2, leaves, nrhs, size), BF)
    return pl.pallas_call(
        lambda *refs: top_kernel(units, *refs),
        out_shape=(jax.ShapeDtypeStruct((nrhs, size), BF), part, part),
        in_specs=[scalars] * 3
        + [whole] * 3
        + [pl.BlockSpec(memory_space=pltpu.HBM)] * 2,
        out_specs=(whole,) * 3,
        scratch_shapes=[
            pltpu.VMEM(rhs.shape, BF),
            pltpu.VMEM(rhs.shape, BF),
            pltpu.VMEM((first_block(count), size, size), BF),
            pltpu.VMEM((groups, leaves, size, size), BF),
            pltpu.SemaphoreType.DMA((count,)),
            pltpu.SemaphoreType.DMA((groups,)),
        ],
        compiler_params=pltpu.CompilerParams(vmem_limit_bytes=32 << 20),
        name="top_solve",
    )(
        at, base, pattern, rhs, updates, inverse,
        pltpu.with_memory_space_constraint(factor, pltpu.HBM),
        pltpu.with_memory_space_constraint(coupled, pltpu.HBM),
    )


def sum_over(value, axis, size):
    value = value.astype(BF)
    got = [value] + [
        lax.ppermute(value, axis, [(i, (i + k) % size) for i in range(size)])
        for k in range(1, size)
    ]
    got = [g.astype(F32) for g in got]
    return (got[0] + got[2]) + (got[1] + got[3])


def build(mesh):
    subs, zs, cores, cols = mesh.devices.shape

    def local(leaf_rhs, leaf_inverse, coupling, pattern, top_rhs, top_inverse, top_factor):
        core = lax.axis_index("core")
        col = lax.axis_index("col")
        row = lax.axis_index("z") * cores + core
        own_rhs = leaf_rhs[0, :, 0]
        own_inverse = jnp.tril(leaf_inverse[0, :, 0])
        coupled = coupling[0, 0, :, 0]
        leaves, nrhs, size = own_rhs.shape
        rows = zs * cores
        assert top_factor.shape[1] == subs

        sub = lax.axis_index("sub")
        column = subs * col + sub
        block = lax.dynamic_index_in_dim(top_factor[0], sub, 0, keepdims=False)
        half = size // 2
        pairs = []
        for i in range(subs * rows * cols):
            s, rest = divmod(i, rows * cols)
            r, c = divmod(rest, cols)
            if r > subs * c + s:
                pairs.append((i, subs * rows * cols - 1 - i))
        moved = lax.ppermute(block[half:], ("sub", "z", "core", "col"), pairs)
        unit = spread_unit(row > column, block[:half], moved, zs)
        ring = lax.all_to_all(unit, "z", 0, 0, tiled=True)

        def units(a, b):
            c, s = divmod(b, subs)
            at = ((s * cols + c) * cores + a % cores) * zs + a // cores
            return at, subs * rows * cols - 1 - at

        top_tri = jnp.tril(top_inverse)

        leaf_forward = jnp.einsum(
            "inb,idb->ind", own_rhs, own_inverse, preferred_element_type=F32
        ).astype(BF)
        swapped = lax.ppermute(leaf_forward, "core", SWAP)
        shared, ring = lax.optimization_barrier(
            (jnp.stack([leaf_forward, swapped]), ring)
        )
        factor = lax.all_gather(ring, ("sub", "col", "core"), axis=0, tiled=True)
        chip = lax.axis_index("z")
        turn = 1 - 2 * core
        other_core = 1 - core

        def base(groups):
            starts = [
                ((chip + away * turn + zs) % zs * cores + part) * leaves
                for away, part in groups
            ]
            return jnp.stack(starts).astype(jnp.int32)

        at = jnp.stack([row, core])
        present = pattern[0, 0, :, 0]
        one = lax.ppermute(shared, ROW, hop(zs, 1))
        two = lax.ppermute(shared, ROW, hop(zs, 2))
        far = lax.ppermute(jnp.concatenate([one, two[:1]]), ROW, hop(zs, 2))
        early = [shared, one, two] + [
            lax.ppermute(part, "core", SWAP) for part in (one, two)
        ]
        late = [far] + [
            lax.ppermute(part, "core", SWAP) for part in (far[:2], far[2:])
        ]
        own, opp = core, other_core
        early_base = base(
            [(0, own), (0, opp), (-1, own), (-1, opp), (-2, own), (-2, opp)]
            + [(1, opp), (1, own), (2, opp), (2, own)]
        )
        late_base = base(
            [(-3, own), (-3, opp), (4, own), (3, opp), (3, own), (4, opp)]
        )
        partial = update_products(early_base, present, early, coupled)
        partial += update_products(late_base, present, late, coupled)
        update = sum_over(sum_over(partial, "sub", subs), "col", cols).astype(BF)
        updates = lax.all_gather(update, ROW, axis=0)

        far_base = base(
            [(-3, 0), (-3, 1), (4, other_core), (3, 0), (3, 1), (4, core)]
        )
        near_base = base(
            [(-1, 0), (-1, 1), (-2, 0), (-2, 1), (0, other_core)]
            + [(1, 0), (1, 1), (2, 0), (2, 1), (0, core)]
        )

        own_top, keep, give = top_solve(
            units, at, far_base, present, top_rhs, updates, top_tri, factor,
            coupled, leaves,
        )
        got = lax.ppermute(give, "core", SWAP)
        sent = (keep.astype(F32) + got.astype(F32)).astype(BF)
        own_late, sent = lax.optimization_barrier((own_top, sent))
        passed = lax.ppermute(sent, ROW, hop(zs, 2)).astype(F32)
        keep, give = near_products(near_base, present, own_late, coupled, leaves)
        near = [
            keep[i:j].astype(F32) + lax.ppermute(give[i:j], "core", SWAP).astype(F32)
            for i, j in ((0, 2), (2, 4), (4, 5))
        ]
        upper = jnp.arange(cores)[:, None, None, None] == core
        one = (near[0] + passed[0:2]).astype(BF)
        two = (near[1] + jnp.where(upper, passed[2][None], 0.0)).astype(BF)
        arrived = lax.ppermute(one, ROW, hop(zs, 1)).astype(F32) + lax.ppermute(
            two, ROW, hop(zs, 2)
        ).astype(F32)
        first = core == 0
        rest = jnp.where(first, arrived[1], arrived[0]).astype(BF)
        kept = near[2][0] + jnp.where(first, arrived[0], arrived[1])
        kept, rest = lax.optimization_barrier((kept, rest))
        back_sums = kept + lax.ppermute(rest, "core", SWAP).astype(F32)
        leaf_residue = (leaf_forward.astype(F32) - back_sums).astype(BF)
        leaf_result = jnp.einsum(
            "inb,ibd->ind", leaf_residue, own_inverse, preferred_element_type=F32
        ).astype(BF)
        return leaf_result[None, :, None], own_top[None]

    return local


def solution(mesh):
    subs, rows, cols = (mesh.shape[name] for name in ("sub", "row", "col"))
    mesh = Mesh(
        mesh.devices.reshape(subs, rows // 2, 2, cols), ("sub", "z", "core", "col")
    )
    placed = (
        P("sub", ROW, "col", None, None),
        P("sub", ROW, "col", None, None),
        P("sub", ROW, None, "col", None, None),
        P("sub", ROW, None, "col"),
        P(),
        P(),
        P(ROW, "col", None, None),
    )
    return jax.shard_map(
        build(mesh),
        mesh=mesh,
        in_specs=placed,
        out_specs=(P("sub", ROW, "col", None, None), P(ROW, None, None)),
        check_vma=False,
    )
```
